32 devices in a mesh: blk: 8 (over z, y), grp: 4 (over x, core).
Axes of the slice: x: 2, y: 2, z: 4, core: 2. Of those that a mesh axis runs over, the one named last changes fastest.
Arguments:
- state: float32 [6, 131072], P(None, ('blk', 'grp')), may hold values from -6 to 6
- mass: float32 [131072], P(('blk', 'grp')), may hold values from 1.5258789e-06 to 3.8146973e-05
- active_index: int32 [8, 32], P('blk'), may hold values from 0 to 16383, as said below
- counts: int32 [8], P('blk'), may hold values from 8 to 32, as said below
Outputs:
- acc_jerk: float32 [6, 256], P(None, 'blk')
- potential: float32 [256], P('blk')
The draws below stay inside these ranges and needn't reach their ends.
Inputs may be any that keep to these rules, and one draw needn't show every extreme that they name: `active_index`: each row holds 32 different star numbers of its slot block; only the first counts[b] entries of row b are active. `counts`: in every draw some slot is full, with 32 active stars.
All inputs are finite; a program needn't handle non-finite values.
Results may differ from the reference program's by a relative error of at most 0.0003.
Values sent between devices are 32-bit elements; how exact they have to be, the bound alone decides.
A program may use at most 64 MiB of HBM per device.

```python
import math
import jax
import jax.numpy as jnp
from jax import lax

F_DEV = 4096
CAP = 32
STARS = 131072
N_BLK = 8
N_GRP = 4


def draw_active_index(key, part):
    keys = jax.random.split(key, N_BLK)
    rows = jax.vmap(lambda single: jax.random.permutation(single, F_DEV * N_GRP)[:CAP])(keys)
    return rows.astype(jnp.int32)


def draw_counts(key, part):
    base = jax.random.randint(key, (N_BLK,), CAP // 4, CAP + 1)
    chosen = jax.random.randint(jax.random.fold_in(key, 7), (), 0, N_BLK)
    return jnp.where(jnp.arange(N_BLK) == chosen, CAP, base).astype(jnp.int32)


def levels(own_key, dims, pieces, smallest, high):
    def one(dim, parts):
        steps = jax.random.uniform(jax.random.fold_in(jax.random.fold_in(own_key, 6), dim), (parts,), jnp.float32, smallest / len(pieces), high / len(pieces))
        return jnp.repeat(jnp.exp(steps), dims[dim] // parts).reshape((-1,) + (1,) * (len(dims) - dim - 1))

    level = one(*pieces[0])
    for cut in pieces[1:]:
        level = level * one(*cut)
    return level


def normal_values(key, extent, scale, limit, pieces=(), held_as=jnp.bfloat16):
    gain = levels(key, extent, pieces, -0.22, 0.18) if pieces else 1.0
    drawn = jax.random.normal(key, extent, jnp.float32) * scale * gain
    return jnp.minimum(jnp.maximum(drawn, -limit), limit).astype(held_as)


def setup_inputs(seed: int = 0) -> dict:
    arg_keys = jax.random.split(jax.random.key(seed), 5)
    state = normal_values(arg_keys[0], (6, STARS), 1.0, 6.0, ((1, 32),), jnp.float32)
    mass = jnp.clip(jnp.exp(math.log(3.814697265625e-05) - 3.218876 * jax.random.uniform(arg_keys[1], (STARS,), jnp.float32) ** levels(arg_keys[1], (STARS,), ((0, 32),), -0.2, 0.2)), 1.5258789289873675e-06, 3.814697265625e-05)
    active_index = draw_active_index(jax.random.fold_in(arg_keys[4], 71), 0)
    counts = draw_counts(jax.random.fold_in(arg_keys[4], 71), 0)
    return dict(state=state, mass=mass, active_index=active_index, counts=counts)


softening = 0.001

def pair_terms(active, field):
    dpos = field[0:3, None, :] - active[0:3, :, None]
    dvel = field[3:6, None, :] - active[3:6, :, None]
    raw = lax.optimization_barrier(jnp.sum(dpos * dpos, axis=0))
    weight = jnp.where(raw == 0.0, 0.0, field[6][None, :])
    inv = lax.rsqrt(raw + softening)
    first = weight * inv
    third = first * inv * inv
    along = lax.optimization_barrier(jnp.sum(dpos * dvel, axis=0))
    fifth = 3.0 * along * third * inv * inv
    accel = lax.optimization_barrier(jnp.sum(third[None] * dpos, axis=-1))
    jerk = lax.optimization_barrier(jnp.sum(third[None] * dvel - fifth[None] * dpos, axis=-1))
    pot = -lax.optimization_barrier(jnp.sum(first, axis=-1))
    return jnp.concatenate([accel, jerk, pot[None]], axis=0)

def reference(state, mass, active_index, counts):
    slot_size = F_DEV * N_GRP
    offsets = jnp.arange(N_BLK, dtype=jnp.int32)[:, None] * slot_size
    global_ids = (active_index + offsets).astype(jnp.int32).reshape(-1)
    active = jnp.take(state, global_ids, axis=1)
    slots = jnp.transpose(active.reshape(6, N_BLK, CAP), (1, 0, 2))
    field = jnp.concatenate([state, mass[None, :]], axis=0)
    blocks = jnp.transpose(field.reshape(7, N_BLK, slot_size), (1, 0, 2))

    def one_slot(rows):

        def add_block(total, block):
            return (total + pair_terms(rows, block), None)
        total, unused = lax.scan(add_block, jnp.zeros((7, CAP), state.dtype), blocks)
        return total
    terms = lax.map(one_slot, slots)
    live = jnp.arange(CAP, dtype=jnp.int32)[None, :] < counts[:, None]
    terms = jnp.where(live[:, None, :], terms, 0.0)
    flat = jnp.transpose(terms, (1, 0, 2)).reshape(7, N_BLK * CAP)
    return (flat[0:6], flat[6])
```

```python
import functools

import jax
import jax.numpy as jnp
from jax import lax
from jax.experimental import pallas as pl
from jax.experimental.pallas import tpu as pltpu
from jax.sharding import PartitionSpec as P

softening = 0.001
LANES = 128
ROWS = 8
CHUNKS = 32
MESH = pl.DeviceIdType.MESH


def pieces(rows):
    out = []
    for _ in range(3):
        piece = rows.astype(jnp.bfloat16).astype(jnp.float32)
        out.append(piece)
        rows = rows - piece
    return jnp.concatenate(out, axis=0)


def turned(x, cap):
    return [x] + [pltpu.roll(x, k * cap, 1) for k in range(1, LANES // cap)]


def by_block(rows, cap):
    block = lax.broadcasted_iota(jnp.int32, rows[0].shape, 1) // cap
    out = rows[0]
    for b in range(1, len(rows)):
        out = jnp.where(block == b, rows[b], out)
    return out


def bits(x, size):
    out = []
    at = 1
    while at < size:
        out.append(lax.rem(lax.div(x, jnp.int32(at)), jnp.int32(2)))
        at *= 2
    return out


def flipped(own, k):
    total = jnp.int32(0)
    for b, bit in enumerate(own):
        if isinstance(k, int):
            total = total + (1 << b) * ((1 - bit) if (k >> b) & 1 else bit)
        else:
            total = total + (1 << b) * lax.rem(bit + lax.div(k, jnp.int32(1 << b)), jnp.int32(2))
    return total


def each(first, last, do):
    if last - first <= 32:
        for i in range(first, last):
            do(i)
    else:
        pl.loop(first, last)(do)


def split(i, size):
    if isinstance(i, int):
        return i // size, i % size
    return lax.div(i, jnp.int32(size)), lax.rem(i, jnp.int32(size))


def group_terms(state_ref, mass_ref, mine, stars):
    def step(base, totals):
        totals = list(totals)
        for k in range(CHUNKS):
            at = pl.ds(pl.multiple_of(base * (CHUNKS * LANES) + k * LANES, LANES), LANES)
            star = [jnp.broadcast_to(state_ref[c : c + 1, at], (ROWS, LANES)) for c in range(6)]
            mass = jnp.broadcast_to(mass_ref[pl.ds(base * CHUNKS + k, 1), :], (ROWS, LANES))
            dx = [star[c] - mine[c] for c in range(3)]
            dv = [star[c] - mine[c] for c in range(3, 6)]
            raw = dx[0] * dx[0] + dx[1] * dx[1] + dx[2] * dx[2]
            weight = jnp.where(raw == 0.0, 0.0, mass)
            inv = lax.rsqrt(raw + softening)
            square = inv * inv
            first = weight * inv
            third = first * square
            along = dx[0] * dv[0] + dx[1] * dv[1] + dx[2] * dv[2]
            ratio = along * square
            for c in range(3):
                pull = third * dx[c]
                totals[c] = totals[c] + pull
                totals[3 + c] = totals[3 + c] + third * dv[c]
                totals[7 + c] = totals[7 + c] + ratio * pull
            totals[6] = totals[6] + first
        return tuple(totals)

    zero = (jnp.zeros((ROWS, LANES), jnp.float32),) * 10
    steps = stars // (CHUNKS * LANES)
    totals = step(0, zero) if steps == 1 else lax.fori_loop(0, steps, step, zero)
    jerk = [totals[3 + c] - 3.0 * totals[7 + c] for c in range(3)]
    return [*totals[:3], *jerk, -totals[6]]


def widen(tall_ref, mine_ref, m, pairs, cap):
    slot, pair = split(m, pairs)
    for h in range(2):
        for c in range(6):
            start = (c % (LANES // cap)) * cap + (2 * pair + h) * ROWS
            block = tall_ref[slot, pl.ds(pl.multiple_of(start, ROWS), ROWS), :]
            column = block[:, c // (LANES // cap) : c // (LANES // cap) + 1]
            mine_ref[m, h, c] = jnp.broadcast_to(column, (ROWS, LANES))


def narrow(acc_ref, line_ref, m):
    line_ref[m] = jnp.sum(acc_ref[m].T, axis=0, keepdims=True)


def kernel(
    n_blk, n_grp, cap, near, state_in, mass_in, picks_in, counts_in, out_ref,
    state_ref, mass_ref, picks_ref, counts_ref, load_sem, part_ref, own_in, list_ref, list_in,
    tall_ref, mine_ref, acc_ref, line_ref, sum_ref, sum_in, own_s, own_r, list_s, list_r, sum_s, sum_r,
):
    blk, grp = lax.axis_index("blk"), lax.axis_index("grp")
    stars = state_ref.shape[1]
    size = LANES // cap
    high = 8 // size
    pairs = cap // (2 * ROWS)
    group = near * n_grp
    tiles = n_blk // near
    everyone = n_blk * n_grp
    blk_bits, grp_bits = bits(blk, n_blk), bits(grp, n_grp)

    def partner(i):
        db, dg = split(i, n_grp)
        return flipped(blk_bits, db), flipped(grp_bits, dg)

    loads = [
        pltpu.make_async_copy(src, dst, load_sem.at[i])
        for i, (src, dst) in enumerate(
            [(picks_in, picks_ref), (state_in, state_ref), (mass_in, mass_ref), (counts_in, counts_ref)]
        )
    ]
    for copy in loads:
        copy.start()

    barrier = pltpu.get_barrier_semaphore()

    def greet(i):
        pl.semaphore_signal(barrier, inc=1, device_id=partner(i), device_id_type=MESH)

    each(1, group, lambda i: greet(group - i))
    for dt in range(1, tiles):
        greet(dt * group)

    def clear(m):
        for h in range(2):
            acc_ref[m, h * 64 : h * 64 + ROWS, :] = jnp.zeros((ROWS, LANES), jnp.float32)

    each(0, pairs * n_blk + 1, clear)

    with jax.named_scope("loadwait"):
        for copy in loads:
            copy.wait()

    picks = jnp.concatenate([picks_ref[...] - grp * stars] * size, axis=1)
    depth = 512
    row = lax.broadcasted_iota(jnp.int32, (depth, LANES), 0)
    found = jnp.zeros((18, LANES), jnp.float32)
    for k in range(stars // depth):
        hot = jnp.where(row + k * depth == picks, 1.0, 0.0).astype(jnp.bfloat16)
        rows = pieces(state_ref[:, k * depth : (k + 1) * depth]).astype(jnp.bfloat16)
        found = found + jnp.dot(rows, hot, preferred_element_type=jnp.float32)
    found = found[0:6] + found[6:12] + found[12:18]
    found = jnp.concatenate([found, jnp.zeros((2, LANES), jnp.float32)], axis=0)
    part = jnp.concatenate(
        [by_block([found[r * size + q :][:1] for q in range(size)], cap) for r in range(high)], axis=0
    )
    part_ref[...] = part
    own_in[0] = part

    with jax.named_scope("barwait"):
        pl.semaphore_wait(barrier, group - 1 + tiles - 1)

    def share(i):
        return pltpu.make_async_remote_copy(
            src_ref=part_ref, dst_ref=own_in.at[i], send_sem=own_s, recv_sem=own_r,
            device_id=partner(i), device_id_type=MESH,
        )

    def pass_on(dt):
        return pltpu.make_async_remote_copy(
            src_ref=list_ref, dst_ref=list_in.at[dt], send_sem=list_s.at[dt], recv_sem=list_r.at[dt],
            device_id=partner(dt * group), device_id_type=MESH,
        )

    def give(i):
        return pltpu.make_async_remote_copy(
            src_ref=sum_ref.at[split(i, n_grp)[0]], dst_ref=sum_in.at[i], send_sem=sum_s, recv_sem=sum_r,
            device_id=partner(i), device_id_type=MESH,
        )

    def whole(ref, count, send_sem, recv_sem):
        span = ref.at[pl.ds(1, count - 1)]
        return pltpu.make_async_remote_copy(
            src_ref=span, dst_ref=span, send_sem=send_sem, recv_sem=recv_sem,
            device_id=partner(1), device_id_type=MESH,
        )

    each(1, group, lambda i: share(group - i).start())

    def turn(slot, listed):
        tall_ref[slot] = jnp.concatenate([listed, jnp.zeros((8 - high, LANES), jnp.float32)], axis=0).T

    def sweep(first, last):
        widen(tall_ref, mine_ref, first * pairs, pairs, cap)

        @pl.loop(first * pairs, last * pairs)
        def _(m):
            mine = [[mine_ref[m, h, c] for c in range(6)] for h in range(2)]
            narrow(acc_ref, line_ref, m)
            widen(tall_ref, mine_ref, jnp.minimum(m + 1, last * pairs - 1), pairs, cap)
            for h in range(2):
                for c, total in enumerate(group_terms(state_ref, mass_ref, mine[h], stars)):
                    acc_ref[m + 1, pl.ds(h * 64 + (7 - c) * ROWS, ROWS), :] = total

        narrow(acc_ref, line_ref, last * pairs)

        def gather(slot):
            for p in range(pairs):
                sum_ref[slot, p : p + 1] = line_ref[slot * pairs + p + 1]

        each(first, last, gather)
        each(first * n_grp + (first == 0), last * n_grp, lambda i: give(i).start())

    with jax.named_scope("sharewait"):
        whole(own_in, group, own_s, own_r).wait_recv()
    with jax.named_scope("lists"):
        lists = []
        for slot in range(near):
            listed = own_in[slot * n_grp]
            for dg in range(1, n_grp):
                listed = listed + own_in[slot * n_grp + dg]
            lists.append(listed)
            list_ref[slot] = listed
        for dt in range(1, tiles):
            pass_on(dt).start()
        for slot in range(near):
            turn(slot, lists[slot])
    with jax.named_scope("near"):
        sweep(1, near)
    for dt in range(1, tiles):
        with jax.named_scope("passwait"):
            pass_on(dt).wait_recv()
        with jax.named_scope("far"):
            for slot in range(near):
                turn(dt * near + slot, list_in[dt, slot])
            cut = dt * near + near // 2
            sweep(cut, (dt + 1) * near)
            sweep(dt * near, cut)
    with jax.named_scope("own"):
        sweep(0, 1)

    sum_in[0] = sum_ref[0]
    with jax.named_scope("takewait"):
        whole(sum_in, everyone, sum_s, sum_r).wait_recv()

    with jax.named_scope("final"):
        sums = [sum_in[k] for k in range(4)]
        for k in range(4, everyone):
            sums[k % 4] = sums[k % 4] + sum_in[k]
        total = (sums[0] + sums[1]) + (sums[2] + sums[3])
        block = lax.broadcasted_iota(jnp.int32, (ROWS, LANES), 1) // ROWS
        table = jnp.zeros((ROWS, LANES), jnp.float32)
        for p in range(pairs):
            line = jnp.broadcast_to(total[p : p + 1], (ROWS, LANES))
            for h in range(2):
                g = 2 * p + h
                moved = pltpu.roll(line, (g * ROWS - h * 64 - 56) % LANES, 1)
                moved = pltpu.roll(moved, 0, 1, stride=ROWS, stride_axis=0)
                table = jnp.where(block == g, moved, table)
        live = lax.broadcasted_iota(jnp.int32, (ROWS, LANES), 1) < counts_ref[...]
        out_ref[...] = jnp.where(live, table, 0.0)

    whole(own_in, group, own_s, own_r).wait_send()
    for dt in range(1, tiles):
        pass_on(dt).wait_send()
    whole(sum_in, everyone, sum_s, sum_r).wait_send()


def part_out(cap, table_ref, out_ref, pot_ref):
    out_ref[...] = table_ref[:6, :cap]
    pot_ref[...] = table_ref[6:7, :cap]


def solution(mesh):
    n_blk, n_grp = mesh.shape["blk"], mesh.shape["grp"]

    def on_device(state, mass, active_index, counts):
        stars, cap = state.shape[1], active_index.shape[1]
        f32 = jnp.float32
        tile = (8 * cap // LANES, LANES)
        everyone = n_blk * n_grp
        pairs = cap // (2 * ROWS)
        near = min(n_blk, LANES // cap)
        tiles = n_blk // near
        sems = pltpu.SemaphoreType.DMA
        vmem = pl.BlockSpec(memory_space=pltpu.VMEM)
        table = pl.pallas_call(
            functools.partial(kernel, n_blk, n_grp, cap, near),
            out_shape=jax.ShapeDtypeStruct((ROWS, LANES), f32),
            in_specs=[pl.BlockSpec(memory_space=pltpu.HBM)] * 3 + [pl.BlockSpec(memory_space=pl.ANY)],
            out_specs=vmem,
            scratch_shapes=[
                pltpu.VMEM((6, stars), f32),
                pltpu.VMEM((stars // LANES, LANES), f32),
                pltpu.VMEM((1, cap), jnp.int32),
                pltpu.VMEM((1, 1), jnp.int32),
                sems((4,)),
                pltpu.VMEM(tile, f32),
                pltpu.VMEM((near * n_grp, *tile), f32),
                pltpu.VMEM((near, *tile), f32),
                pltpu.VMEM((tiles, near, *tile), f32),
                pltpu.VMEM((n_blk, LANES, 8), f32),
                pltpu.VMEM((n_blk * pairs, 2, 6, ROWS, LANES), f32),
                pltpu.VMEM((n_blk * pairs + 1, LANES, LANES), f32),
                pltpu.VMEM((n_blk * pairs + 1, 1, LANES), f32),
                pltpu.VMEM((n_blk, *tile), f32),
                pltpu.VMEM((everyone, *tile), f32),
                sems(()), sems(()), sems((tiles,)), sems((tiles,)), sems(()), sems(()),
            ],
            compiler_params=pltpu.CompilerParams(
                collective_id=0, has_side_effects=True, vmem_limit_bytes=40 * 1024 * 1024
            ),
        )(*(
            pltpu.with_memory_space_constraint(x, pltpu.HBM)
            for x in (state, mass.reshape(stars // LANES, LANES), active_index)
        ), counts.reshape(1, 1))
        out, pot = pl.pallas_call(
            functools.partial(part_out, cap),
            out_shape=(jax.ShapeDtypeStruct((6, cap), f32), jax.ShapeDtypeStruct((1, cap), f32)),
            in_specs=[vmem],
            out_specs=(vmem, vmem),
            compiler_params=pltpu.CompilerParams(vmem_limit_bytes=1024 * 1024),
        )(table)
        return out, pot.reshape(cap)

    placed = (P(None, ("blk", "grp")), P(("blk", "grp")), P("blk", None), P("blk"))
    return jax.shard_map(
        on_device, mesh=mesh, in_specs=placed, out_specs=(P(None, "blk"), P("blk")), check_vma=False
    )
```
